128 devices in a mesh: row: 8 (over x, core), col: 16 (over z, y).
Axes of the slice: x: 4, y: 4, z: 4, core: 2. Of those that a mesh axis runs over, the one named last changes fastest.
Arguments:
- model_init: float32 [2, 2, 16, 16384], P(None, None, None, 'col'), may hold values from -2 to 2
- observed: float32 [2, 2, 16, 32768], P(None, None, None, ('row', 'col')), may hold values from -6 to 6
- left_bases: bfloat16 [128, 64, 2, 96, 2, 256], P(('row', 'col')), may hold values from -0.078125 to 0.078125
- right_bases: bfloat16 [128, 64, 2, 96, 2, 256], P('row', 'col'), may hold values from -0.078125 to 0.078125
- tile_ranks: int32 [128, 64, 2], P('row', 'col'), may hold values from 8 to 96
- gate_start: int32 [16, 32768], P(None, ('row', 'col')), may hold values from 0 to 31
- gate_stop: int32 [16, 32768], P(None, ('row', 'col')), may hold values from 32 to 64
Outputs:
- model_final: float32 [2, 2, 16, 16384], P(None, None, None, 'col')
- residual_final: float32 [2, 2, 16, 32768], P(None, None, None, ('row', 'col'))
The draws below stay inside these ranges and needn't reach their ends.
All inputs are finite; a program needn't handle non-finite values.
Results may differ from the reference program's by a relative error of at most 0.009.
Values may be sent and summed in bfloat16 or wider, within the bound.
No kernel may reach another device: no remote copies, remote signals or barrier semaphores. Data moves between devices by JAX's collectives and lax.ppermute only.
A program may use at most 128 MiB of HBM per device.

```python
import math
import jax
import jax.numpy as jnp
from jax import lax

NV = 16
TILE = 256
RMAX = 96
F = 2
NT = 64
ITERS = 2
TROWS = 128
TCOLS = 64
NR = 32768
NS = 16384


def set_ends(array, key, smallest, high):
    dims = array.shape
    place = [jax.random.randint(jax.random.fold_in(key, axis), (), 0, dims[axis]) for axis in range(len(dims))]
    array = array.at[tuple(place)].set(smallest)
    longest = dims.index(max(dims))
    place[longest] = (place[longest] + 1) % dims[longest]
    return array.at[tuple(place)].set(high)


def block_levels(stream_key, shape, split, smallest, largest):
    factor_of = 1.0
    for axis_at, shards_of in split:
        heights = jax.random.uniform(jax.random.fold_in(jax.random.fold_in(stream_key, 6), axis_at), (shards_of,), jnp.float32, smallest / len(split), largest / len(split))
        factor_of = factor_of * jnp.repeat(jnp.exp(heights), shape[axis_at] // shards_of).reshape((-1,) + (1,) * (len(shape) - 1 - axis_at))
    return factor_of


def bell_draw(key, extent, deviation, most, split=(), kind=jnp.bfloat16):
    array = jax.random.normal(key, extent, jnp.float32) * deviation
    if len(split) > 0:
        array = block_levels(key, extent, split, -0.22, 0.18) * array
    return jnp.clip(array, min=-most, max=most).astype(kind)


def setup_inputs(seed: int = 0) -> dict:
    key_list = jax.random.split(jax.random.key(seed), 8)
    return {
        "model_init": bell_draw(key_list[0], (2, F, NV, NS), 0.3, 2.0, ((3, 16),), jnp.float32),
        "observed": bell_draw(key_list[1], (2, F, NV, NR), 1.0, 6.0, ((3, 128),), jnp.float32),
        "left_bases": bell_draw(key_list[2], (TROWS, TCOLS, F, RMAX, 2, TILE), (TILE * (TROWS + TCOLS) // 8) ** -0.5, 0.078125, ((0, 128),)),
        "right_bases": bell_draw(key_list[3], (TROWS, TCOLS, F, RMAX, 2, TILE), (TILE * (TROWS + TCOLS) // 8) ** -0.5, 0.078125, ((0, 8), (1, 16))),
        "tile_ranks": set_ends(jax.random.randint(key_list[4], (TROWS, TCOLS, F), RMAX // 12, RMAX + 1), jax.random.fold_in(key_list[4], 1), RMAX // 12, RMAX).astype(jnp.int32),
        "gate_start": set_ends(jax.random.randint(key_list[5], (NV, NR), 0, NT // 2), jax.random.fold_in(key_list[5], 1), 0, (NT // 2) - 1).astype(jnp.int32),
        "gate_stop": set_ends(jax.random.randint(key_list[6], (NV, NR), NT // 2, NT + 1), jax.random.fold_in(key_list[6], 1), NT // 2, NT).astype(jnp.int32),
    }


step_length = 0.8


def time_table(samples):
    sample_times = jnp.arange(samples, dtype=jnp.float32)[:, None]
    freq_bins = (3.0 + 5.0 * jnp.arange(F, dtype=jnp.float32))[None, :]
    phases = 2.0 * math.pi * sample_times * freq_bins / samples
    return jnp.concatenate([jnp.cos(phases), -jnp.sin(phases)], axis=1)


def apply_gate(field, gate_start, gate_stop):
    transform = time_table(NT)
    flattened = field.reshape(2 * F, -1)
    signal = jnp.dot(transform, flattened, precision=lax.Precision.HIGHEST)
    sample_index = jnp.arange(NT, dtype=jnp.int32)[:, None, None]
    window = ((sample_index >= gate_start[None]) & (sample_index < gate_stop[None])).astype(jnp.float32)
    windowed = signal * window.reshape(NT, -1)
    returned = jnp.dot(transform.T, windowed, precision=lax.Precision.HIGHEST) * (2.0 / NT)
    return returned.reshape(field.shape)


def pair_rows(field):
    real_part, imag_part = field[0], field[1]
    upper_pair = jnp.stack([real_part, imag_part], axis=3)
    lower_pair = jnp.stack([imag_part, -real_part], axis=3)
    joined = jnp.stack([upper_pair, lower_pair], axis=1)
    return jnp.transpose(joined, (3, 0, 1, 2, 4, 5))


def combine(stacked):
    real_part = stacked[:, :, 0, :, 0] - stacked[:, :, 1, :, 1]
    imag_part = stacked[:, :, 0, :, 1] + stacked[:, :, 1, :, 0]
    joined = jnp.stack([real_part, imag_part], axis=0)
    joined = jnp.transpose(joined, (0, 2, 3, 1, 4))
    return joined.reshape(joined.shape[0], joined.shape[1], joined.shape[2], -1)


def reference(model_init, observed, left_bases, right_bases, tile_ranks, gate_start, gate_stop):
    rank_index = jnp.arange(RMAX, dtype=jnp.int32)
    tile_rows = jnp.arange(TROWS, dtype=jnp.int32)

    def rank_mask(tile_row):
        return (rank_index[None, None, :] < tile_ranks[tile_row][:, :, None]).astype(jnp.float32)

    def forward(estimate):
        low_model = estimate.astype(jnp.bfloat16).reshape(2, F, NV, TCOLS, TILE)
        paired = pair_rows(low_model).astype(jnp.float32)

        def one_row(tile_row):
            right_tile = right_bases[tile_row].astype(jnp.float32)
            left_tile = left_bases[tile_row].astype(jnp.float32)
            coefficients = jnp.einsum("jfavcs,jfkcs->jfavk", paired, right_tile)
            coefficients = coefficients * rank_mask(tile_row)[:, :, None, None, :]
            coefficients = lax.optimization_barrier(coefficients.astype(jnp.bfloat16)).astype(jnp.float32)
            return jnp.einsum("jfavk,jfkcn->favcn", coefficients, left_tile)

        modeled = lax.map(one_row, tile_rows)
        return combine(modeled)

    def adjoint(residual):
        low_residual = residual.astype(jnp.bfloat16).reshape(2, F, NV, TROWS, TILE)
        paired = pair_rows(low_residual).astype(jnp.float32)

        def add_row(running, tile_row):
            right_tile = right_bases[tile_row].astype(jnp.float32)
            left_tile = left_bases[tile_row].astype(jnp.float32)
            coefficients = jnp.einsum("favcn,jfkcn->jfavk", paired[tile_row], left_tile)
            coefficients = lax.optimization_barrier(coefficients.astype(jnp.bfloat16)).astype(jnp.float32)
            coefficients = coefficients * rank_mask(tile_row)[:, :, None, None, :]
            return running + jnp.einsum("jfavk,jfkcs->jfavcs", coefficients, right_tile), None

        zeros = jnp.zeros((TCOLS, F, 2, NV, 2, TILE), jnp.float32)
        running, _ = lax.scan(add_row, zeros, tile_rows)
        return combine(running)

    estimate = model_init
    for iteration in range(ITERS):
        residual = apply_gate(forward(estimate) - observed, gate_start, gate_stop)
        estimate = estimate - step_length * adjoint(residual)
    residual = apply_gate(forward(estimate) - observed, gate_start, gate_stop)
    return estimate, residual
```

```python
import math

import jax
import jax.numpy as jnp
from jax import lax
from jax.experimental import pallas as pl
from jax.experimental.pallas import tpu as pltpu
from jax.sharding import PartitionSpec as P

NV = 16
TILE = 256
RMAX = 96
F = 2
NT = 64
ITERS = 2
WIDE = F * RMAX * 2
ROWS = F * 2 * NV

step_length = 0.8


def lane_facts(rows):
    lane = lax.broadcasted_iota(jnp.int32, (rows, WIDE), 1)
    return lane % 2 == 0, lane < WIDE // 2, lane


def project(field, basis, even, first):
    z = lax.dot_general(field, basis, (((1,), (1,)), ((), ())), preferred_element_type=jnp.float32)
    real = jnp.where(first, z[0:NV], z[2 * NV : 3 * NV])
    imag = jnp.where(first, z[NV : 2 * NV], z[3 * NV :])
    ahead = pltpu.roll(imag, WIDE - 1, 1)
    behind = pltpu.roll(imag, 1, 1)
    return real + jnp.where(even, ahead, -behind)


def expand(packed, basis, even, first):
    wide = packed.astype(jnp.float32)
    ahead = pltpu.roll(wide, WIDE - 1, 1)
    behind = pltpu.roll(wide, 1, 1)
    swapped = jnp.where(even, -ahead, behind)
    zero = jnp.zeros_like(wide)
    left = jnp.concatenate(
        [
            jnp.where(first, wide, zero),
            jnp.where(first, swapped, zero),
            jnp.where(first, zero, wide),
            jnp.where(first, zero, swapped),
        ],
        axis=0,
    ).astype(jnp.bfloat16)
    return jnp.dot(left, basis, preferred_element_type=jnp.float32)


def forward_kernel(model_ref, basis_ref, ranks_ref, out_ref):
    even, first, lane = lane_facts(NV)
    rank_of_lane = jnp.where(first, lane, lane - WIDE // 2) // 2
    for j in range(4):
        field = jnp.concatenate(
            [model_ref[a, f, :, j * TILE : (j + 1) * TILE] for f in range(F) for a in range(2)], axis=0
        ).astype(jnp.bfloat16)

        def one(i, carry):
            tile = i * 4 + j
            x = project(field, basis_ref[tile], even, first)
            limit = jnp.where(first, ranks_ref[tile, 0], ranks_ref[tile, 1])
            x = jnp.where(rank_of_lane < limit, x, 0.0)
            out_ref[tile] = x.astype(jnp.bfloat16)
            return carry

        lax.fori_loop(0, 16, one, 0, unroll=4)


def gate(re0, im0, re1, im1, start, stop):
    outs = [jnp.zeros_like(re0) for _ in range(4)]
    for t in range(NT):
        rows = []
        for f in range(F):
            phase = 2.0 * math.pi * ((3 + 5 * f) * t % NT) / NT
            rows += [math.cos(phase), -math.sin(phase)]
        signal = re0 * rows[0] + im0 * rows[1] + re1 * rows[2] + im1 * rows[3]
        signal = jnp.where((start <= t) & (stop > t), signal, 0.0)
        outs = [o + signal * r for o, r in zip(outs, rows)]
    return [o * (2.0 / NT) for o in outs]


def residual_parts(got_ref, basis_ref, observed_ref, start_ref, stop_ref, total_ref):
    even, first, _ = lane_facts(NV)
    total_ref[...] = jnp.zeros_like(total_ref)

    def one(j, carry):
        total_ref[...] += expand(got_ref[j], basis_ref[j], even, first)
        return carry

    lax.fori_loop(0, 64, one, 0, unroll=4)
    parts = [
        total_ref[(2 * f + a) * NV : (2 * f + a + 1) * NV] - observed_ref[a, f] for f in range(F) for a in range(2)
    ]
    return gate(*parts, start_ref[...], stop_ref[...])


def middle_kernel(got_ref, basis_ref, observed_ref, start_ref, stop_ref, out_ref, total_ref):
    parts = residual_parts(got_ref, basis_ref, observed_ref, start_ref, stop_ref, total_ref)
    field = jnp.concatenate(parts, axis=0).astype(jnp.bfloat16)
    even, first, _ = lane_facts(NV)

    def one(j, carry):
        out_ref[j] = project(field, basis_ref[j], even, first).astype(jnp.bfloat16)
        return carry

    lax.fori_loop(0, 64, one, 0, unroll=4)


def last_kernel(got_ref, basis_ref, observed_ref, start_ref, stop_ref, out_ref, total_ref):
    parts = residual_parts(got_ref, basis_ref, observed_ref, start_ref, stop_ref, total_ref)
    for f in range(F):
        for a in range(2):
            out_ref[a, f] = parts[2 * f + a]


def gradient_kernel(got_ref, basis_ref, ranks_ref, out_ref, total_ref):
    even, first, lane = lane_facts(NV)
    rank_of_lane = jnp.where(first, lane, lane - WIDE // 2) // 2
    for j in range(4):
        total_ref[...] = jnp.zeros_like(total_ref)

        def one(i, carry):
            tile = i * 4 + j
            limit = jnp.where(first, ranks_ref[tile, 0], ranks_ref[tile, 1])
            kept = jnp.where(rank_of_lane < limit, got_ref[tile].astype(jnp.float32), 0.0)
            total_ref[...] += expand(kept, basis_ref[tile], even, first)
            return carry

        lax.fori_loop(0, 16, one, 0, unroll=4)
        for f in range(F):
            for a in range(2):
                row = (2 * f + a) * NV
                out_ref[a, f, :, j * TILE : (j + 1) * TILE] = total_ref[row : row + NV]


VMEM = pl.BlockSpec(memory_space=pltpu.VMEM)
SMEM = pl.BlockSpec(memory_space=pltpu.SMEM)
PACKED = jax.ShapeDtypeStruct((64, NV, WIDE), jnp.bfloat16)
TOTAL = pltpu.VMEM((ROWS, TILE), jnp.float32)
PARAMS = pltpu.CompilerParams(vmem_limit_bytes=40 * 1024 * 1024)


def call(kernel, specs, out, scratch):
    return pl.pallas_call(
        kernel,
        out_shape=out,
        in_specs=specs,
        out_specs=VMEM,
        scratch_shapes=scratch,
        compiler_params=PARAMS,
        name=kernel.__name__,
    )


def exchange(packed):
    parts = packed.reshape(16, 4, NV, WIDE)
    return lax.all_to_all(parts, "col", 0, 0, tiled=True).reshape(64, NV, WIDE)


def row_sum(local):
    low = local.astype(jnp.bfloat16).astype(jnp.float32)
    for step in (1, 2, 4):
        other = lax.ppermute(low.astype(jnp.bfloat16), "row", [(d, d ^ step) for d in range(8)])
        low = low.astype(jnp.bfloat16).astype(jnp.float32) + other.astype(jnp.float32)
    return low


def shards(model_init, observed, left_bases, right_bases, tile_ranks, gate_start, gate_stop):
    left = left_bases.reshape(64, WIDE, TILE)
    right = right_bases.reshape(64, WIDE, TILE)
    ranks = tile_ranks.reshape(64, F)
    forward = call(forward_kernel, [VMEM, VMEM, SMEM], PACKED, [])
    middle = call(middle_kernel, [VMEM] * 5, PACKED, [TOTAL])
    last = call(last_kernel, [VMEM] * 5, jax.ShapeDtypeStruct((2, F, NV, TILE), jnp.float32), [TOTAL])
    gradient = call(
        gradient_kernel, [VMEM, VMEM, SMEM], jax.ShapeDtypeStruct((2, F, NV, 1024), jnp.float32), [TOTAL]
    )
    estimate = model_init
    for iteration in range(ITERS):
        got = exchange(forward(estimate, right, ranks))
        back = exchange(middle(got, left, observed, gate_start, gate_stop))
        estimate = estimate - step_length * row_sum(gradient(back, right, ranks))
    got = exchange(forward(estimate, right, ranks))
    return estimate, last(got, left, observed, gate_start, gate_stop)


def solution(mesh):
    placed = (
        P(None, None, None, "col"),
        P(None, None, None, ("row", "col")),
        P(("row", "col"), None, None, None, None, None),
        P("row", "col", None, None, None, None),
        P("row", "col", None),
        P(None, ("row", "col")),
        P(None, ("row", "col")),
    )
    return jax.shard_map(
        shards,
        mesh=mesh,
        in_specs=placed,
        out_specs=(P(None, None, None, "col"), P(None, None, None, ("row", "col"))),
        check_vma=False,
    )
```

```python
import math

import jax
import jax.numpy as jnp
from jax import lax
from jax.experimental import pallas as pl
from jax.experimental.pallas import tpu as pltpu
from jax.sharding import PartitionSpec as P

NV = 16
TILE = 256
RMAX = 96
F = 2
NT = 64
ITERS = 2
LANES = 128
HALVES = TILE // LANES
PAIRS = RMAX * 2
WIDE = F * PAIRS
ROWS = F * 2 * NV
GROUPS = 8
GROUP = 8

step_length = 0.8


def start_fetch(raw_ref, held_ref, sems):
    for group in range(GROUPS):
        for copy in fetches(raw_ref, held_ref, sems, group):
            copy.start()


def fetches(raw_ref, held_ref, sems, group):
    copies = []
    raw_ref = raw_ref.reshape(*raw_ref.shape[:-3], PAIRS, TILE)
    for half in range(HALVES):
        lanes = pl.ds(half * LANES, LANES)
        if len(raw_ref.shape) == 5:
            column, part = group // 2, group % 2
            source = raw_ref.at[pl.ds(part * GROUP, GROUP), column, :, :, lanes]
        else:
            source = raw_ref.at[pl.ds(group * GROUP, GROUP), :, :, lanes]
        copies.append(pltpu.make_async_copy(source, held_ref.at[half, group], sems.at[group, half]))
    return copies


def wait_fetch(raw_ref, held_ref, sems, group):
    for copy in fetches(raw_ref, held_ref, sems, group):
        copy.wait()


def lane_facts():
    lane = lax.broadcasted_iota(jnp.int32, (NV, WIDE), 1)
    first = lane < PAIRS
    rank = jnp.where(first, lane, lane - PAIRS) // 2
    return lane % 2 == 0, first, rank


def repeat_field(real, imag):
    return jnp.concatenate([real] * GROUP + [imag] * GROUP, axis=0).astype(jnp.bfloat16)


def project(wide_of, basis_ref, group):
    spot = lax.broadcasted_iota(jnp.int32, (PAIRS, LANES), 1) // NV
    even = lax.broadcasted_iota(jnp.int32, (PAIRS, LANES), 0) % 2 == 0
    blocks = []
    for f in range(F):
        rows = jnp.concatenate(
            [basis_ref[half, group, :, f].reshape(GROUP * PAIRS, LANES) for half in range(HALVES)], axis=1
        )
        z = lax.dot_general(rows, wide_of(f), (((1,), (1,)), ((), ())), preferred_element_type=jnp.float32)
        real, imag = z[0:PAIRS, :LANES], z[0:PAIRS, LANES:]
        for p in range(1, GROUP):
            here = spot == p
            real = jnp.where(here, z[p * PAIRS : (p + 1) * PAIRS, :LANES], real)
            imag = jnp.where(here, z[p * PAIRS : (p + 1) * PAIRS, LANES:], imag)
        ahead = pltpu.roll(imag, PAIRS - 1, 0)
        behind = pltpu.roll(imag, 1, 0)
        blocks.append(real + jnp.where(even, ahead, -behind))
    return jnp.concatenate(blocks, axis=0).T


def expand(packed, basis, even, first):
    wide = packed.astype(jnp.float32)
    ahead = pltpu.roll(wide, WIDE - 1, 1)
    behind = pltpu.roll(wide, 1, 1)
    swapped = jnp.where(even, -ahead, behind)
    zero = jnp.zeros_like(wide)
    left = jnp.concatenate(
        [
            jnp.where(first, wide, zero),
            jnp.where(first, swapped, zero),
            jnp.where(first, zero, wide),
            jnp.where(first, zero, swapped),
        ],
        axis=0,
    ).astype(jnp.bfloat16)
    return jnp.dot(left, basis, preferred_element_type=jnp.float32)


def tile_of(basis_ref, group, p):
    return jnp.concatenate([basis_ref[half, group, p].reshape(WIDE, LANES) for half in range(HALVES)], axis=1)


def rows_by_pair(held_ref):
    return held_ref


def forward_kernel(model_ref, raw_ref, ranks_ref, out_ref, held_ref, wide_ref, sems):
    start_fetch(raw_ref, held_ref, sems)
    basis_ref = rows_by_pair(held_ref)
    _, first, rank = lane_facts()
    for j in range(4):
        for f in range(F):
            real, imag = [model_ref[a, f, :, j * TILE : (j + 1) * TILE] for a in range(2)]
            wide_ref[j, f] = repeat_field(real, imag)

    def one(group, carry):
        wait_fetch(raw_ref, held_ref, sems, group)
        j = group // 2
        x = project(lambda f: wide_ref[j, f], basis_ref, group)
        for p in range(GROUP):
            tile = ((group % 2) * GROUP + p) * 4 + j
            limit = jnp.where(first, ranks_ref[tile, 0], ranks_ref[tile, 1])
            mine = jnp.where(rank < limit, x[p * NV : (p + 1) * NV], 0.0)
            out_ref[tile] = mine.astype(jnp.bfloat16)
        return carry

    lax.fori_loop(0, GROUPS, one, 0)


def gate(re0, im0, re1, im1, start, stop):
    outs = [jnp.zeros_like(re0) for _ in range(4)]
    for t in range(NT):
        rows = []
        for f in range(F):
            phase = 2.0 * math.pi * ((3 + 5 * f) * t % NT) / NT
            rows += [math.cos(phase), -math.sin(phase)]
        signal = re0 * rows[0] + im0 * rows[1] + re1 * rows[2] + im1 * rows[3]
        signal = jnp.where((start <= t) & (stop > t), signal, 0.0)
        outs = [o + signal * r for o, r in zip(outs, rows)]
    return [o * (2.0 / NT) for o in outs]


def residual_parts(got_ref, raw_ref, observed_ref, start_ref, stop_ref, held_ref, total_ref, sems):
    start_fetch(raw_ref, held_ref, sems)
    basis_ref = rows_by_pair(held_ref)
    even, first, _ = lane_facts()
    total_ref[...] = jnp.zeros_like(total_ref)

    def one(group, carry):
        wait_fetch(raw_ref, held_ref, sems, group)
        total = total_ref[...]
        for p in range(GROUP):
            total += expand(got_ref[group * GROUP + p], tile_of(basis_ref, group, p), even, first)
        total_ref[...] = total
        return carry

    lax.fori_loop(0, GROUPS, one, 0)
    parts = [
        total_ref[(2 * f + a) * NV : (2 * f + a + 1) * NV] - observed_ref[a, f] for f in range(F) for a in range(2)
    ]
    return gate(*parts, start_ref[...], stop_ref[...])


def middle_kernel(got_ref, raw_ref, observed_ref, start_ref, stop_ref, out_ref, held_ref, total_ref, wide_ref, sems):
    parts = residual_parts(got_ref, raw_ref, observed_ref, start_ref, stop_ref, held_ref, total_ref, sems)
    basis_ref = rows_by_pair(held_ref)
    for f in range(F):
        wide_ref[f] = repeat_field(parts[2 * f], parts[2 * f + 1])

    def one(group, carry):
        x = project(lambda f: wide_ref[f], basis_ref, group).astype(jnp.bfloat16)
        for p in range(GROUP):
            out_ref[group * GROUP + p] = x[p * NV : (p + 1) * NV]
        return carry

    lax.fori_loop(0, GROUPS, one, 0)


def last_kernel(got_ref, raw_ref, observed_ref, start_ref, stop_ref, out_ref, held_ref, total_ref, sems):
    parts = residual_parts(got_ref, raw_ref, observed_ref, start_ref, stop_ref, held_ref, total_ref, sems)
    for f in range(F):
        for a in range(2):
            out_ref[a, f] = parts[2 * f + a]


def gradient_kernel(got_ref, raw_ref, ranks_ref, out_ref, held_ref, sems):
    start_fetch(raw_ref, held_ref, sems)
    basis_ref = rows_by_pair(held_ref)
    even, first, rank = lane_facts()
    for j in range(4):

        def one(part, total):
            group = 2 * j + part
            wait_fetch(raw_ref, held_ref, sems, group)
            for p in range(GROUP):
                tile = (part * GROUP + p) * 4 + j
                limit = jnp.where(first, ranks_ref[tile, 0], ranks_ref[tile, 1])
                kept = jnp.where(rank < limit, got_ref[tile].astype(jnp.float32), 0.0)
                total += expand(kept, tile_of(basis_ref, group, p), even, first)
            return total

        total = lax.fori_loop(0, 2, one, jnp.zeros((ROWS, TILE), jnp.float32))
        for f in range(F):
            for a in range(2):
                row = (2 * f + a) * NV
                out_ref[a, f, :, j * TILE : (j + 1) * TILE] = total[row : row + NV]


VMEM = pl.BlockSpec(memory_space=pltpu.VMEM)
SMEM = pl.BlockSpec(memory_space=pltpu.SMEM)
HBM = pl.BlockSpec(memory_space=pltpu.HBM)
PACKED = jax.ShapeDtypeStruct((64, NV, WIDE), jnp.bfloat16)
HELD = pltpu.VMEM((HALVES, GROUPS, GROUP, F, PAIRS, LANES), jnp.bfloat16)
TOTAL = pltpu.VMEM((ROWS, TILE), jnp.float32)
SEMS = pltpu.SemaphoreType.DMA((GROUPS, HALVES))


def wide(*lead):
    return pltpu.VMEM((*lead, F, TILE, TILE), jnp.bfloat16)


def call(kernel, specs, out, scratch):
    return pl.pallas_call(
        kernel,
        out_shape=out,
        in_specs=specs,
        out_specs=VMEM,
        scratch_shapes=scratch,
        compiler_params=pltpu.CompilerParams(vmem_limit_bytes=40 * 1024 * 1024),
        name=kernel.__name__,
    )


def exchange(packed):
    parts = packed.reshape(16, 4, NV, WIDE)
    return lax.all_to_all(parts, "col", 0, 0, tiled=True).reshape(64, NV, WIDE)


def row_sum(local):
    low = local.astype(jnp.bfloat16).astype(jnp.float32)
    for step in (1, 2, 4):
        other = lax.ppermute(low.astype(jnp.bfloat16), "row", [(d, d ^ step) for d in range(8)])
        low = low.astype(jnp.bfloat16).astype(jnp.float32) + other.astype(jnp.float32)
    return low


def shards(model_init, observed, left_bases, right_bases, tile_ranks, gate_start, gate_stop):
    left = pltpu.with_memory_space_constraint(left_bases.reshape(left_bases.shape[1:]), pltpu.HBM)
    right = pltpu.with_memory_space_constraint(right_bases, pltpu.HBM)
    ranks = tile_ranks.reshape(64, F)
    forward = call(forward_kernel, [VMEM, HBM, SMEM], PACKED, [HELD, wide(4), SEMS])
    middle = call(middle_kernel, [VMEM, HBM] + [VMEM] * 3, PACKED, [HELD, TOTAL, wide(), SEMS])
    last = call(
        last_kernel,
        [VMEM, HBM] + [VMEM] * 3,
        jax.ShapeDtypeStruct((2, F, NV, TILE), jnp.float32),
        [HELD, TOTAL, SEMS],
    )
    gradient = call(
        gradient_kernel, [VMEM, HBM, SMEM], jax.ShapeDtypeStruct((2, F, NV, 1024), jnp.float32), [HELD, SEMS]
    )
    estimate = model_init
    for iteration in range(ITERS):
        got = exchange(forward(estimate, right, ranks))
        back = exchange(middle(got, left, observed, gate_start, gate_stop))
        estimate = estimate - step_length * row_sum(gradient(back, right, ranks))
    got = exchange(forward(estimate, right, ranks))
    return estimate, last(got, left, observed, gate_start, gate_stop)


def solution(mesh):
    placed = (
        P(None, None, None, "col"),
        P(None, None, None, ("row", "col")),
        P(("row", "col"), None, None, None, None, None),
        P("row", "col", None, None, None, None),
        P("row", "col", None),
        P(None, ("row", "col")),
        P(None, ("row", "col")),
    )
    return jax.shard_map(
        shards,
        mesh=mesh,
        in_specs=placed,
        out_specs=(P(None, None, None, "col"), P(None, None, None, ("row", "col"))),
        check_vma=False,
    )
```

```python
import math

import jax
import jax.numpy as jnp
from jax import lax
from jax.experimental import pallas as pl
from jax.experimental.pallas import tpu as pltpu
from jax.sharding import PartitionSpec as P

NV = 16
TILE = 256
RMAX = 96
F = 2
NT = 64
ITERS = 2
LANES = 128
HALVES = TILE // LANES
PAIRS = RMAX * 2
WIDE = F * PAIRS
ROWS = F * 2 * NV
GROUPS = 8
GROUP = 8

step_length = 0.8


def start_fetch(raw_ref, held_ref, sems):
    for group in range(GROUPS):
        for copy in fetches(raw_ref, held_ref, sems, group):
            copy.start()


def fetches(raw_ref, held_ref, sems, group):
    copies = []
    raw_ref = raw_ref.reshape(*raw_ref.shape[:-3], PAIRS, TILE)
    for half in range(HALVES):
        lanes = pl.ds(half * LANES, LANES)
        if len(raw_ref.shape) == 5:
            column, part = group // 2, group % 2
            source = raw_ref.at[pl.ds(part * GROUP, GROUP), column, :, :, lanes]
        else:
            source = raw_ref.at[pl.ds(group * GROUP, GROUP), :, :, lanes]
        copies.append(pltpu.make_async_copy(source, held_ref.at[half, group], sems.at[group, half]))
    return copies


def wait_fetch(raw_ref, held_ref, sems, group):
    for copy in fetches(raw_ref, held_ref, sems, group):
        copy.wait()


def lane_facts():
    lane = lax.broadcasted_iota(jnp.int32, (NV, WIDE), 1)
    first = lane < PAIRS
    rank = jnp.where(first, lane, lane - PAIRS) // 2
    return lane % 2 == 0, first, rank


def repeat_field(real, imag):
    return jnp.concatenate([real] * GROUP + [imag] * GROUP, axis=0).T.astype(jnp.bfloat16)


def project(wide_of, basis_ref, group):
    spot = lax.broadcasted_iota(jnp.int32, (PAIRS, LANES), 1) // NV
    even = lax.broadcasted_iota(jnp.int32, (PAIRS, LANES), 0) % 2 == 0
    blocks = []
    for f in range(F):
        rows = jnp.concatenate(
            [basis_ref[half, group, :, f].reshape(GROUP * PAIRS, LANES) for half in range(HALVES)], axis=1
        )
        z = jnp.dot(rows, wide_of(f), preferred_element_type=jnp.float32)
        real, imag = z[0:PAIRS, :LANES], z[0:PAIRS, LANES:]
        for p in range(1, GROUP):
            here = spot == p
            real = jnp.where(here, z[p * PAIRS : (p + 1) * PAIRS, :LANES], real)
            imag = jnp.where(here, z[p * PAIRS : (p + 1) * PAIRS, LANES:], imag)
        ahead = pltpu.roll(imag, PAIRS - 1, 0)
        behind = pltpu.roll(imag, 1, 0)
        blocks.append(real + jnp.where(even, ahead, -behind))
    return jnp.concatenate(blocks, axis=0).T


def expand(packed, basis, even, first):
    wide = packed.astype(jnp.float32)
    ahead = pltpu.roll(wide, WIDE - 1, 1)
    behind = pltpu.roll(wide, 1, 1)
    swapped = jnp.where(even, -ahead, behind)
    zero = jnp.zeros_like(wide)
    left = jnp.concatenate(
        [
            jnp.where(first, wide, zero),
            jnp.where(first, swapped, zero),
            jnp.where(first, zero, wide),
            jnp.where(first, zero, swapped),
        ],
        axis=0,
    ).astype(jnp.bfloat16)
    return jnp.dot(left, basis, preferred_element_type=jnp.float32)


def tile_of(basis_ref, group, p):
    return jnp.concatenate([basis_ref[half, group, p].reshape(WIDE, LANES) for half in range(HALVES)], axis=1)


def rows_by_pair(held_ref):
    return held_ref


def forward_kernel(model_ref, raw_ref, ranks_ref, out_ref, held_ref, wide_ref, sems):
    start_fetch(raw_ref, held_ref, sems)
    basis_ref = rows_by_pair(held_ref)
    _, first, rank = lane_facts()
    for j in range(4):
        for f in range(F):
            real, imag = [model_ref[a, f, :, j * TILE : (j + 1) * TILE] for a in range(2)]
            wide_ref[j, f] = repeat_field(real, imag)

    def one(group, carry):
        wait_fetch(raw_ref, held_ref, sems, group)
        j = group // 2
        x = project(lambda f: wide_ref[j, f], basis_ref, group)
        for p in range(GROUP):
            tile = ((group % 2) * GROUP + p) * 4 + j
            limit = jnp.where(first, ranks_ref[tile, 0], ranks_ref[tile, 1])
            mine = jnp.where(rank < limit, x[p * NV : (p + 1) * NV], 0.0)
            out_ref[tile] = mine.astype(jnp.bfloat16)
        return carry

    lax.fori_loop(0, GROUPS, one, 0, unroll=2)


def gate(re0, im0, re1, im1, start, stop):
    outs = [jnp.zeros_like(re0) for _ in range(4)]
    for t in range(NT):
        rows = []
        for f in range(F):
            phase = 2.0 * math.pi * ((3 + 5 * f) * t % NT) / NT
            rows += [math.cos(phase), -math.sin(phase)]
        signal = re0 * rows[0] + im0 * rows[1] + re1 * rows[2] + im1 * rows[3]
        signal = jnp.where((start <= t) & (stop > t), signal, 0.0)
        outs = [o + signal * r for o, r in zip(outs, rows)]
    return [o * (2.0 / NT) for o in outs]


def residual_parts(got_ref, raw_ref, observed_ref, start_ref, stop_ref, held_ref, total_ref, sems):
    start_fetch(raw_ref, held_ref, sems)
    basis_ref = rows_by_pair(held_ref)
    even, first, _ = lane_facts()
    total_ref[...] = jnp.zeros_like(total_ref)

    def one(group, carry):
        wait_fetch(raw_ref, held_ref, sems, group)
        total = total_ref[...]
        for p in range(GROUP):
            total += expand(got_ref[group * GROUP + p], tile_of(basis_ref, group, p), even, first)
        total_ref[...] = total
        return carry

    lax.fori_loop(0, GROUPS, one, 0)
    parts = [
        total_ref[(2 * f + a) * NV : (2 * f + a + 1) * NV] - observed_ref[a, f] for f in range(F) for a in range(2)
    ]
    return gate(*parts, start_ref[...], stop_ref[...])


def middle_kernel(got_ref, raw_ref, observed_ref, start_ref, stop_ref, out_ref, held_ref, total_ref, wide_ref, sems):
    parts = residual_parts(got_ref, raw_ref, observed_ref, start_ref, stop_ref, held_ref, total_ref, sems)
    basis_ref = rows_by_pair(held_ref)
    for f in range(F):
        wide_ref[f] = repeat_field(parts[2 * f], parts[2 * f + 1])

    def one(group, carry):
        x = project(lambda f: wide_ref[f], basis_ref, group).astype(jnp.bfloat16)
        for p in range(GROUP):
            out_ref[group * GROUP + p] = x[p * NV : (p + 1) * NV]
        return carry

    lax.fori_loop(0, GROUPS, one, 0, unroll=2)


def last_kernel(got_ref, raw_ref, observed_ref, start_ref, stop_ref, out_ref, held_ref, total_ref, sems):
    parts = residual_parts(got_ref, raw_ref, observed_ref, start_ref, stop_ref, held_ref, total_ref, sems)
    for f in range(F):
        for a in range(2):
            out_ref[a, f] = parts[2 * f + a]


def gradient_kernel(got_ref, raw_ref, ranks_ref, out_ref, held_ref, sems):
    start_fetch(raw_ref, held_ref, sems)
    basis_ref = rows_by_pair(held_ref)
    even, first, rank = lane_facts()
    for j in range(4):

        def one(part, total):
            group = 2 * j + part
            wait_fetch(raw_ref, held_ref, sems, group)
            for p in range(GROUP):
                tile = (part * GROUP + p) * 4 + j
                limit = jnp.where(first, ranks_ref[tile, 0], ranks_ref[tile, 1])
                kept = jnp.where(rank < limit, got_ref[tile].astype(jnp.float32), 0.0)
                total += expand(kept, tile_of(basis_ref, group, p), even, first)
            return total

        total = lax.fori_loop(0, 2, one, jnp.zeros((ROWS, TILE), jnp.float32))
        for f in range(F):
            for a in range(2):
                row = (2 * f + a) * NV
                out_ref[a, f, :, j * TILE : (j + 1) * TILE] = total[row : row + NV]


VMEM = pl.BlockSpec(memory_space=pltpu.VMEM)
SMEM = pl.BlockSpec(memory_space=pltpu.SMEM)
HBM = pl.BlockSpec(memory_space=pltpu.HBM)
PACKED = jax.ShapeDtypeStruct((64, NV, WIDE), jnp.bfloat16)
HELD = pltpu.VMEM((HALVES, GROUPS, GROUP, F, PAIRS, LANES), jnp.bfloat16)
TOTAL = pltpu.VMEM((ROWS, TILE), jnp.float32)
SEMS = pltpu.SemaphoreType.DMA((GROUPS, HALVES))


def wide(*lead):
    return pltpu.VMEM((*lead, F, TILE, TILE), jnp.bfloat16)


def call(kernel, specs, out, scratch):
    return pl.pallas_call(
        kernel,
        out_shape=out,
        in_specs=specs,
        out_specs=VMEM,
        scratch_shapes=scratch,
        compiler_params=pltpu.CompilerParams(vmem_limit_bytes=40 * 1024 * 1024),
        name=kernel.__name__,
    )


def exchange(packed):
    parts = packed.reshape(16, 4, NV, WIDE)
    return lax.all_to_all(parts, "col", 0, 0, tiled=True).reshape(64, NV, WIDE)


def row_sum(local):
    low = local.astype(jnp.bfloat16).astype(jnp.float32)
    for step in (1, 2, 6):
        other = lax.ppermute(low.astype(jnp.bfloat16), "row", [(d, d ^ step) for d in range(8)])
        low = low.astype(jnp.bfloat16).astype(jnp.float32) + other.astype(jnp.float32)
    return low


def shards(model_init, observed, left_bases, right_bases, tile_ranks, gate_start, gate_stop):
    left = pltpu.with_memory_space_constraint(left_bases.reshape(left_bases.shape[1:]), pltpu.HBM)
    right = pltpu.with_memory_space_constraint(right_bases, pltpu.HBM)
    ranks = tile_ranks.reshape(64, F)
    forward = call(forward_kernel, [VMEM, HBM, SMEM], PACKED, [HELD, wide(4), SEMS])
    middle = call(middle_kernel, [VMEM, HBM] + [VMEM] * 3, PACKED, [HELD, TOTAL, wide(), SEMS])
    last = call(
        last_kernel,
        [VMEM, HBM] + [VMEM] * 3,
        jax.ShapeDtypeStruct((2, F, NV, TILE), jnp.float32),
        [HELD, TOTAL, SEMS],
    )
    gradient = call(
        gradient_kernel, [VMEM, HBM, SMEM], jax.ShapeDtypeStruct((2, F, NV, 1024), jnp.float32), [HELD, SEMS]
    )
    estimate = model_init
    for iteration in range(ITERS):
        got = exchange(forward(estimate, right, ranks))
        back = exchange(middle(got, left, observed, gate_start, gate_stop))
        estimate = estimate - step_length * row_sum(gradient(back, right, ranks))
    got = exchange(forward(estimate, right, ranks))
    return estimate, last(got, left, observed, gate_start, gate_stop)


def solution(mesh):
    placed = (
        P(None, None, None, "col"),
        P(None, None, None, ("row", "col")),
        P(("row", "col"), None, None, None, None, None),
        P("row", "col", None, None, None, None),
        P("row", "col", None),
        P(None, ("row", "col")),
        P(None, ("row", "col")),
    )
    return jax.shard_map(
        shards,
        mesh=mesh,
        in_specs=placed,
        out_specs=(P(None, None, None, "col"), P(None, None, None, ("row", "col"))),
        check_vma=False,
    )
```

```python
import math

import jax
import jax.numpy as jnp
from jax import lax
from jax.experimental import pallas as pl
from jax.experimental.pallas import tpu as pltpu
from jax.sharding import PartitionSpec as P

NV = 16
TILE = 256
RMAX = 96
F = 2
NT = 64
ITERS = 2
LANES = 128
HALVES = TILE // LANES
PAIRS = RMAX * 2
WIDE = F * PAIRS
ROWS = F * 2 * NV
GROUPS = 8
GROUP = 8

step_length = 0.8


def start_fetch(raw_ref, held_ref, sems):
    for group in range(GROUPS):
        for copy in fetches(raw_ref, held_ref, sems, group):
            copy.start()


def fetches(raw_ref, held_ref, sems, group):
    copies = []
    raw_ref = raw_ref.reshape(*raw_ref.shape[:-3], PAIRS, TILE)
    for half in range(HALVES):
        lanes = pl.ds(half * LANES, LANES)
        if len(raw_ref.shape) == 5:
            column, part = group // 2, group % 2
            source = raw_ref.at[pl.ds(part * GROUP, GROUP), column, :, :, lanes]
        else:
            source = raw_ref.at[pl.ds(group * GROUP, GROUP), :, :, lanes]
        copies.append(pltpu.make_async_copy(source, held_ref.at[half, group], sems.at[group, half]))
    return copies


def wait_fetch(raw_ref, held_ref, sems, group):
    for copy in fetches(raw_ref, held_ref, sems, group):
        copy.wait()


def lane_facts():
    lane = lax.broadcasted_iota(jnp.int32, (NV, WIDE), 1)
    first = lane < PAIRS
    rank = jnp.where(first, lane, lane - PAIRS) // 2
    return lane % 2 == 0, first, rank


def repeat_field(real, imag):
    return jnp.concatenate([real] * GROUP + [imag] * GROUP, axis=0).T.astype(jnp.bfloat16)


def project(wide_of, basis_ref, group):
    spot = lax.broadcasted_iota(jnp.int32, (PAIRS, LANES), 1) // NV
    even = lax.broadcasted_iota(jnp.int32, (PAIRS, LANES), 0) % 2 == 0
    blocks = []
    for f in range(F):
        rows = jnp.concatenate(
            [basis_ref[half, group, :, f].reshape(GROUP * PAIRS, LANES) for half in range(HALVES)], axis=1
        )
        z = jnp.dot(rows, wide_of(f), preferred_element_type=jnp.float32)
        real, imag = z[0:PAIRS, :LANES], z[0:PAIRS, LANES:]
        for p in range(1, GROUP):
            here = spot == p
            real = jnp.where(here, z[p * PAIRS : (p + 1) * PAIRS, :LANES], real)
            imag = jnp.where(here, z[p * PAIRS : (p + 1) * PAIRS, LANES:], imag)
        ahead = pltpu.roll(imag, PAIRS - 1, 0)
        behind = pltpu.roll(imag, 1, 0)
        blocks.append(real + jnp.where(even, ahead, -behind))
    return jnp.concatenate(blocks, axis=0).T


def expand(packed, basis, even, first):
    wide = packed.astype(jnp.float32)
    ahead = pltpu.roll(wide, WIDE - 1, 1)
    behind = pltpu.roll(wide, 1, 1)
    swapped = jnp.where(even, -ahead, behind)
    zero = jnp.zeros_like(wide)
    left = jnp.concatenate(
        [
            jnp.where(first, wide, zero),
            jnp.where(first, swapped, zero),
            jnp.where(first, zero, wide),
            jnp.where(first, zero, swapped),
        ],
        axis=0,
    ).astype(jnp.bfloat16)
    return jnp.dot(left, basis, preferred_element_type=jnp.float32)


def tile_of(basis_ref, group, p):
    return jnp.concatenate([basis_ref[half, group, p].reshape(WIDE, LANES) for half in range(HALVES)], axis=1)


def rows_by_pair(held_ref):
    return held_ref


def first_kernel(source_ref, raw_ref, ranks_ref, out_ref, held_ref, wide_ref, sems, model_ref, model_sem):
    copy = pltpu.make_async_copy(source_ref, model_ref, model_sem)
    copy.start()
    forward_kernel(model_ref, raw_ref, ranks_ref, out_ref, held_ref, wide_ref, sems, copy.wait)


def forward_kernel(model_ref, raw_ref, ranks_ref, out_ref, held_ref, wide_ref, sems, ready=None):
    start_fetch(raw_ref, held_ref, sems)
    if ready is not None:
        ready()
    basis_ref = rows_by_pair(held_ref)
    _, first, rank = lane_facts()
    for j in range(4):
        for f in range(F):
            real, imag = [model_ref[a, f, :, j * TILE : (j + 1) * TILE] for a in range(2)]
            wide_ref[j, f] = repeat_field(real, imag)

    def one(group, carry):
        wait_fetch(raw_ref, held_ref, sems, group)
        j = group // 2
        x = project(lambda f: wide_ref[j, f], basis_ref, group)
        for p in range(GROUP):
            tile = ((group % 2) * GROUP + p) * 4 + j
            limit = jnp.where(first, ranks_ref[tile, 0], ranks_ref[tile, 1])
            mine = jnp.where(rank < limit, x[p * NV : (p + 1) * NV], 0.0)
            out_ref[tile] = mine.astype(jnp.bfloat16)
        return carry

    lax.fori_loop(0, GROUPS, one, 0, unroll=2)


def gate(re0, im0, re1, im1, start, stop):
    outs = [jnp.zeros_like(re0) for _ in range(4)]
    for t in range(NT):
        rows = []
        for f in range(F):
            phase = 2.0 * math.pi * ((3 + 5 * f) * t % NT) / NT
            rows += [math.cos(phase), -math.sin(phase)]
        signal = re0 * rows[0] + im0 * rows[1] + re1 * rows[2] + im1 * rows[3]
        signal = jnp.where((start <= t) & (stop > t), signal, 0.0)
        outs = [o + signal * r for o, r in zip(outs, rows)]
    return [o * (2.0 / NT) for o in outs]


def residual_parts(got_ref, raw_ref, observed_ref, start_ref, stop_ref, held_ref, total_ref, sems):
    start_fetch(raw_ref, held_ref, sems)
    basis_ref = rows_by_pair(held_ref)
    even, first, _ = lane_facts()
    total_ref[...] = jnp.zeros_like(total_ref)

    def one(group, carry):
        wait_fetch(raw_ref, held_ref, sems, group)
        total = total_ref[...]
        for p in range(GROUP):
            total += expand(got_ref[group * GROUP + p], tile_of(basis_ref, group, p), even, first)
        total_ref[...] = total
        return carry

    lax.fori_loop(0, GROUPS, one, 0)
    parts = [
        total_ref[(2 * f + a) * NV : (2 * f + a + 1) * NV] - observed_ref[a, f] for f in range(F) for a in range(2)
    ]
    return gate(*parts, start_ref[...], stop_ref[...])


def middle_kernel(got_ref, raw_ref, observed_ref, start_ref, stop_ref, out_ref, held_ref, total_ref, wide_ref, sems):
    parts = residual_parts(got_ref, raw_ref, observed_ref, start_ref, stop_ref, held_ref, total_ref, sems)
    basis_ref = rows_by_pair(held_ref)
    for f in range(F):
        wide_ref[f] = repeat_field(parts[2 * f], parts[2 * f + 1])

    def one(group, carry):
        x = project(lambda f: wide_ref[f], basis_ref, group).astype(jnp.bfloat16)
        for p in range(GROUP):
            out_ref[group * GROUP + p] = x[p * NV : (p + 1) * NV]
        return carry

    lax.fori_loop(0, GROUPS, one, 0, unroll=2)


def last_kernel(got_ref, raw_ref, observed_ref, start_ref, stop_ref, out_ref, held_ref, total_ref, sems):
    parts = residual_parts(got_ref, raw_ref, observed_ref, start_ref, stop_ref, held_ref, total_ref, sems)
    for f in range(F):
        for a in range(2):
            out_ref[a, f] = parts[2 * f + a]


def gradient_kernel(got_ref, raw_ref, ranks_ref, out_ref, held_ref, sems):
    start_fetch(raw_ref, held_ref, sems)
    basis_ref = rows_by_pair(held_ref)
    even, first, rank = lane_facts()
    for j in range(4):

        def one(part, total):
            group = 2 * j + part
            wait_fetch(raw_ref, held_ref, sems, group)
            for p in range(GROUP):
                tile = (part * GROUP + p) * 4 + j
                limit = jnp.where(first, ranks_ref[tile, 0], ranks_ref[tile, 1])
                kept = jnp.where(rank < limit, got_ref[tile].astype(jnp.float32), 0.0)
                total += expand(kept, tile_of(basis_ref, group, p), even, first)
            return total

        total = lax.fori_loop(0, 2, one, jnp.zeros((ROWS, TILE), jnp.float32))
        for f in range(F):
            for a in range(2):
                row = (2 * f + a) * NV
                out_ref[a, f, :, j * TILE : (j + 1) * TILE] = total[row : row + NV]


VMEM = pl.BlockSpec(memory_space=pltpu.VMEM)
SMEM = pl.BlockSpec(memory_space=pltpu.SMEM)
HBM = pl.BlockSpec(memory_space=pltpu.HBM)
PACKED = jax.ShapeDtypeStruct((64, NV, WIDE), jnp.bfloat16)
HELD = pltpu.VMEM((HALVES, GROUPS, GROUP, F, PAIRS, LANES), jnp.bfloat16)
TOTAL = pltpu.VMEM((ROWS, TILE), jnp.float32)
SEMS = pltpu.SemaphoreType.DMA((GROUPS, HALVES))


def wide(*lead):
    return pltpu.VMEM((*lead, F, TILE, TILE), jnp.bfloat16)


def call(kernel, specs, out, scratch):
    return pl.pallas_call(
        kernel,
        out_shape=out,
        in_specs=specs,
        out_specs=VMEM,
        scratch_shapes=scratch,
        compiler_params=pltpu.CompilerParams(vmem_limit_bytes=40 * 1024 * 1024),
        name=kernel.__name__,
    )


def exchange(packed):
    parts = packed.reshape(16, 4, NV, WIDE)
    return lax.all_to_all(parts, "col", 0, 0, tiled=True).reshape(64, NV, WIDE)


def row_sum(local):
    low = local.astype(jnp.bfloat16).astype(jnp.float32)
    for step in (1, 2, 6):
        other = lax.ppermute(low.astype(jnp.bfloat16), "row", [(d, d ^ step) for d in range(8)])
        low = low.astype(jnp.bfloat16).astype(jnp.float32) + other.astype(jnp.float32)
    return low


def shards(model_init, observed, left_bases, right_bases, tile_ranks, gate_start, gate_stop):
    left = pltpu.with_memory_space_constraint(left_bases.reshape(left_bases.shape[1:]), pltpu.HBM)
    right = pltpu.with_memory_space_constraint(right_bases, pltpu.HBM)
    ranks = tile_ranks.reshape(64, F)
    forward = call(forward_kernel, [VMEM, HBM, SMEM], PACKED, [HELD, wide(4), SEMS])
    first = call(
        first_kernel,
        [HBM, HBM, SMEM],
        PACKED,
        [HELD, wide(4), SEMS, pltpu.VMEM((2, F, NV, 1024), jnp.float32), pltpu.SemaphoreType.DMA],
    )
    middle = call(middle_kernel, [VMEM, HBM] + [VMEM] * 3, PACKED, [HELD, TOTAL, wide(), SEMS])
    last = call(
        last_kernel,
        [VMEM, HBM] + [VMEM] * 3,
        jax.ShapeDtypeStruct((2, F, NV, TILE), jnp.float32),
        [HELD, TOTAL, SEMS],
    )
    gradient = call(
        gradient_kernel, [VMEM, HBM, SMEM], jax.ShapeDtypeStruct((2, F, NV, 1024), jnp.float32), [HELD, SEMS]
    )
    estimate = model_init
    for iteration in range(ITERS):
        if iteration == 0:
            sent = first(pltpu.with_memory_space_constraint(model_init, pltpu.HBM), right, ranks)
        else:
            sent = forward(estimate, right, ranks)
        got = exchange(sent)
        back = exchange(middle(got, left, observed, gate_start, gate_stop))
        estimate = estimate - step_length * row_sum(gradient(back, right, ranks))
    got = exchange(forward(estimate, right, ranks))
    return estimate, last(got, left, observed, gate_start, gate_stop)


def solution(mesh):
    placed = (
        P(None, None, None, "col"),
        P(None, None, None, ("row", "col")),
        P(("row", "col"), None, None, None, None, None),
        P("row", "col", None, None, None, None),
        P("row", "col", None),
        P(None, ("row", "col")),
        P(None, ("row", "col")),
    )
    return jax.shard_map(
        shards,
        mesh=mesh,
        in_specs=placed,
        out_specs=(P(None, None, None, "col"), P(None, None, None, ("row", "col"))),
        check_vma=False,
    )
```
